256 devices in a mesh: sp: 8 (over z), dp: 32 (over x, y, core).
Axes of the slice: x: 4, y: 4, z: 8, core: 2. Of those that a mesh axis runs over, the one named last changes fastest.
Arguments:
- hidden_states: bfloat16 [32, 2048, 8192], P('dp', 'sp'), may hold values from -6 to 6
- queries: bfloat16 [32, 2048, 4096], P('dp', 'sp'), may hold values from -360 to 360
- norm_gain: bfloat16 [8192], replicated, may hold values from 0.5 to 1.5
- key_value_matrix: bfloat16 [8192, 1024], P('dp'), may hold values from -0.0625 to 0.0625
- trace_offsets: int32 [32, 9], P('dp'), may hold values from 0 to 2048, as said below
- token_order: int32 [32, 2048], P('dp'), may hold values from 0 to 2047, each once within a row
Outputs:
- attended: bfloat16 [32, 2048, 4096], P('dp', 'sp')
The draws below stay inside these ranges and needn't reach their ends.
Inputs may be any that keep to these rules, and one draw needn't show every extreme that they name: Each row rises strictly from 0 to 2048; trace t of pack p holds the positions from trace_offsets[p, t] to trace_offsets[p, t + 1] - 1. `token_order`: each row is a permutation of the 2048 positions of its pack.
All inputs are finite; a program needn't handle non-finite values.
Results may differ from the reference program's by a relative error of at most 0.0034.
The reference program's roundings to bfloat16 on the way count: a program that leaves them out, or rounds other values in their place, can miss the bound.
Values may be sent and summed in bfloat16 or wider, within the bound.
No kernel may reach another device: no remote copies, remote signals or barrier semaphores. Data moves between devices by JAX's collectives and lax.ppermute only.
A program may use at most 128 MiB of HBM per device.

```python
import math
import jax
import jax.numpy as jnp
from jax import lax

MODEL_WIDTH = 8192
QUERY_HEADS = 32
KEY_VALUE_HEADS = 4
HEAD_SIZE = 128
TRACES = 8
PACK_TOKENS = 2048
PACKS = 32


def draw_trace_offsets(key, part):

    def one_pack(subkey):
        cuts = jax.random.permutation(subkey, PACK_TOKENS - 1)[:TRACES - 1] + 1
        cuts = jnp.sort(cuts.astype(jnp.int32))
        return jnp.concatenate([jnp.zeros((1,), jnp.int32), cuts, jnp.full((1,), PACK_TOKENS, jnp.int32)])
    return jax.vmap(one_pack)(jax.random.split(jax.random.fold_in(key, 11), PACKS))


def draw_queries(key, part):
    base = jnp.clip(jax.random.normal(jax.random.fold_in(key, 3), (PACKS, PACK_TOKENS, QUERY_HEADS, HEAD_SIZE), jnp.float32), -6.0, 6.0)
    return base.reshape(PACKS, PACK_TOKENS, QUERY_HEADS * HEAD_SIZE).astype(jnp.bfloat16)


def block_scale(key, dims, shards, smallest, high):
    loudness = 1.0
    for position, shards_of in shards:
        draws = jax.random.uniform(jax.random.fold_in(jax.random.fold_in(key, 6), position), (shards_of,), jnp.float32, smallest / len(shards), high / len(shards))
        loudness = loudness * jnp.repeat(jnp.exp(draws), dims[position] // shards_of).reshape((-1,) + (1,) * (len(dims) - 1 - position))
    return loudness


def centred(rng, shape, scale, bound, shards=(), kind=jnp.bfloat16):
    level = block_scale(rng, shape, shards, -0.22, 0.18) if shards else 1.0
    drawn = jax.random.normal(rng, shape, jnp.float32) * scale * level
    return jnp.minimum(jnp.maximum(drawn, -bound), bound).astype(kind)


def setup_inputs(seed: int = 0) -> dict:
    keys = jax.random.split(jax.random.key(seed), 7)
    return {
        "hidden_states": centred(keys[0], (PACKS, PACK_TOKENS, MODEL_WIDTH), 1.0, 6.0, ((0, 32), (1, 8))),
        "queries": draw_queries(jax.random.fold_in(keys[6], 71), 0),
        "norm_gain": jnp.clip(1.0 + 0.1 * jax.random.normal(keys[2], (MODEL_WIDTH,), jnp.float32), 0.5, 1.5).astype(jnp.bfloat16),
        "key_value_matrix": centred(keys[3], (MODEL_WIDTH, KEY_VALUE_HEADS * 2 * HEAD_SIZE), MODEL_WIDTH ** -0.5, 0.0625, ((0, 32),)),
        "trace_offsets": draw_trace_offsets(jax.random.fold_in(keys[6], 71), 0),
        "token_order": jax.vmap(lambda own: jax.random.permutation(own, PACK_TOKENS))(jax.random.split(keys[5], PACKS)).reshape((PACKS, PACK_TOKENS)).astype(jnp.int32),
    }


EPSILON = 1e-05
ROPE_BASE = 500000.0

def locate(positions, starts):
    inside = starts[None, :] <= positions[:, None]
    trace_ids = lax.optimization_barrier(jnp.sum(inside.astype(jnp.int32), axis=1)) - 1
    begin = lax.optimization_barrier(jnp.max(jnp.where(inside, starts[None, :], 0), axis=1))
    return (trace_ids.astype(jnp.int32), (positions - begin).astype(jnp.int32))

def rotate(vectors, within):
    half = vectors.shape[-1] // 2
    index = jnp.arange(half, dtype=jnp.float32)
    freqs = jnp.exp(index * (-2.0 * math.log(ROPE_BASE) / vectors.shape[-1]))
    angles = within.astype(jnp.float32)[:, None] * freqs[None, :]
    cosine = jnp.cos(angles)[:, None, :]
    sine = jnp.sin(angles)[:, None, :]
    first = vectors[..., :half]
    second = vectors[..., half:]
    return jnp.concatenate([first * cosine - second * sine, second * cosine + first * sine], axis=-1)

def normalize(rows, gain):
    value_rows = rows.astype(jnp.float32)
    scale = lax.rsqrt(lax.optimization_barrier(jnp.mean(value_rows * value_rows, axis=-1, keepdims=True)) + EPSILON)
    return (value_rows * scale * gain.astype(jnp.float32)).astype(jnp.bfloat16)

def reference(hidden_states, queries, norm_gain, key_value_matrix, trace_offsets, token_order):

    def one_pack(operands):
        rows, query_rows, starts, positions = operands
        normed = normalize(rows, norm_gain)
        projected_rows = jnp.dot(normed, key_value_matrix, preferred_element_type=jnp.float32)
        trace_ids, within = locate(positions, starts)
        key_value_pairs = projected_rows.reshape(PACK_TOKENS, KEY_VALUE_HEADS, 2, HEAD_SIZE)
        key_rows = rotate(key_value_pairs[:, :, 0], within).astype(jnp.bfloat16).astype(jnp.float32)
        value_rows = key_value_pairs[:, :, 1].astype(jnp.bfloat16).astype(jnp.float32)
        head_slices = rotate(query_rows.astype(jnp.float32).reshape(PACK_TOKENS, QUERY_HEADS, HEAD_SIZE), within).astype(jnp.bfloat16)
        head_slices = head_slices.reshape(PACK_TOKENS, KEY_VALUE_HEADS, QUERY_HEADS // KEY_VALUE_HEADS, HEAD_SIZE)
        width = min(512, PACK_TOKENS)

        def block(block_index):
            first_row = block_index * width
            query_block = lax.dynamic_slice_in_dim(head_slices, first_row, width, 0).astype(jnp.float32)
            block_ids = lax.dynamic_slice_in_dim(trace_ids, first_row, width, 0)
            block_positions = lax.dynamic_slice_in_dim(positions, first_row, width, 0)
            scores = jnp.einsum('bgpd,kgd->gpbk', query_block, key_rows) / math.sqrt(HEAD_SIZE)
            mask = (block_ids[:, None] == trace_ids[None, :]) & (positions[None, :] <= block_positions[:, None])
            scores = jnp.where(mask, scores, -1e+30)
            peak = lax.optimization_barrier(jnp.max(scores, axis=-1, keepdims=True))
            expo = jnp.where(mask, jnp.exp(scores - peak), 0.0)
            totals = lax.optimization_barrier(jnp.sum(expo, axis=-1))
            weights = expo.astype(jnp.bfloat16).astype(jnp.float32)
            mixed = jnp.einsum('gpbk,kgd->bgpd', weights, value_rows)
            result = mixed / jnp.transpose(totals, (2, 0, 1))[..., None]
            return result.astype(jnp.bfloat16).reshape(width, QUERY_HEADS * HEAD_SIZE)
        outputs = lax.map(block, jnp.arange(PACK_TOKENS // width, dtype=jnp.int32))
        return outputs.reshape(PACK_TOKENS, QUERY_HEADS * HEAD_SIZE)
    return lax.map(one_pack, (hidden_states, queries, trace_offsets, token_order))
```

```python
import functools
import math

import jax
import jax.numpy as jnp
from jax import lax
from jax.experimental import pallas as pl
from jax.experimental.pallas import tpu as pltpu
from jax.sharding import PartitionSpec as P

QUERY_HEADS = 32
KEY_VALUE_HEADS = 4
HEAD_SIZE = 128
EPSILON = 1e-05
ROPE_BASE = 500000.0

ROWS = 256
WIDTH = 8192
PACK = 2048
GROUP = QUERY_HEADS // KEY_VALUE_HEADS
SIDE = 4
CHIPS = SIDE * SIDE
RING = 8
CHUNKS = 2
CHUNK_HEADS = KEY_VALUE_HEADS // CHUNKS
CHUNK_COLUMNS = CHUNK_HEADS * 2 * HEAD_SIZE
HIDDEN = -1e30


VMEM = pl.BlockSpec(memory_space=pltpu.VMEM)
SMEM = pl.BlockSpec(memory_space=pltpu.SMEM)


def plane_permutation(phase, shift):
    pairs = []
    for x in range(SIDE):
        for y in range(SIDE):
            for core in range(2):
                along_x = (core == 0) == (phase == 0)
                tx = (x + shift) % SIDE if along_x else x
                ty = y if along_x else (y + shift) % SIDE
                pairs.append(((x * SIDE + y) * 2 + core, (tx * SIDE + ty) * 2 + core))
    return pairs


def plane_shift(array, phase, shift):
    return lax.ppermute(array, "dp", plane_permutation(phase, shift))


def partner_swap(array):
    return lax.ppermute(array, "dp", [(d, d ^ 1) for d in range(2 * CHIPS)])


def ring_shift(array, shift):
    return lax.ppermute(array, "sp", [(s, (s + shift) % RING) for s in range(RING)])


def cost(flops, nbytes, transcendentals=0):
    return pl.CostEstimate(flops=flops, bytes_accessed=nbytes, transcendentals=transcendentals)


def project_kernel(first, counts, has_start, table, own, partner, *refs):
    blocks = refs[: len(counts)]
    rest = refs[len(counts) :]
    out_own, out_partner = rest[-2:]
    if has_start:
        total = [rest[0][...], rest[1][...]]
    else:
        total = [jnp.zeros(out_own.shape, jnp.float32)] * 2
    index = first
    for ref, count in zip(blocks, counts):
        for i in range(count):
            chip = table[index]
            index += 1
            features = pl.ds(pl.multiple_of(chip * ROWS, ROWS), ROWS)
            weight = ref[i * ROWS : (i + 1) * ROWS, :]
            for j, x in enumerate((own, partner)):
                total[j] = total[j] + jnp.dot(
                    x[:, features], weight, preferred_element_type=jnp.float32
                )
    out_own[...] = total[0]
    out_partner[...] = total[1]


def project(table, own, partner, blocks, first, start=None):
    counts = tuple(b.shape[0] // ROWS for b in blocks)
    columns = blocks[0].shape[1]
    n = sum(counts)
    shape = jax.ShapeDtypeStruct((ROWS, columns), jnp.float32)
    extra = () if start is None else tuple(start)
    return pl.pallas_call(
        functools.partial(project_kernel, first, counts, start is not None),
        out_shape=(shape, shape),
        in_specs=[SMEM] + [VMEM] * (2 + len(blocks) + len(extra)),
        out_specs=(VMEM, VMEM),
        cost_estimate=cost(4 * n * ROWS * ROWS * columns, 2 * n * ROWS * (columns + 2 * ROWS)),
        name="project",
    )(table, own, partner, *blocks, *extra)


def turned(u, cosine, sine):
    return u * cosine + pltpu.roll(u, HEAD_SIZE // 2, 1) * sine


def keys_kernel(mine, theirs, cosine, sine, out):
    cos = cosine[...]
    sin = sine[...]
    for h in range(CHUNK_HEADS):
        a = 2 * h * HEAD_SIZE
        key = mine[:, a : a + HEAD_SIZE] + theirs[:, a : a + HEAD_SIZE]
        a += HEAD_SIZE
        value = mine[:, a : a + HEAD_SIZE] + theirs[:, a : a + HEAD_SIZE]
        out[:ROWS, h * HEAD_SIZE : (h + 1) * HEAD_SIZE] = turned(key, cos, sin).astype(jnp.bfloat16)
        out[ROWS + h * HEAD_SIZE : ROWS + (h + 1) * HEAD_SIZE, :] = value.T.astype(jnp.bfloat16)


def finish_keys(mine, theirs, cosine, sine):
    return pl.pallas_call(
        keys_kernel,
        out_shape=jax.ShapeDtypeStruct((2 * ROWS, ROWS), jnp.bfloat16),
        in_specs=[VMEM] * 4,
        out_specs=VMEM,
        cost_estimate=cost(8 * ROWS * CHUNK_COLUMNS, 10 * ROWS * CHUNK_COLUMNS),
        name="finish_keys",
    )(mine, theirs, cosine, sine)


def queries_kernel(queries, cosine, sine, out):
    u = queries[...].astype(jnp.float32)
    out[...] = turned(u, cosine[...], sine[...]).T.astype(jnp.bfloat16)


def rotate_queries(queries, cosine, sine):
    whole = pl.BlockSpec((ROWS, HEAD_SIZE), lambda h: (0, 0))
    return pl.pallas_call(
        queries_kernel,
        grid=(QUERY_HEADS,),
        out_shape=jax.ShapeDtypeStruct((QUERY_HEADS * HEAD_SIZE, ROWS), jnp.bfloat16),
        in_specs=[pl.BlockSpec((ROWS, HEAD_SIZE), lambda h: (0, h)), whole, whole],
        out_specs=pl.BlockSpec((HEAD_SIZE, ROWS), lambda h: (h, 0)),
        cost_estimate=cost(4 * ROWS * QUERY_HEADS * HEAD_SIZE, 4 * ROWS * QUERY_HEADS * HEAD_SIZE),
        name="rotate_queries",
    )(queries, cosine, sine)


def bias_kernel(positions, own, begin, out):
    keys = positions[...]
    kept = (keys >= begin[...]) & (keys <= own[...])
    out[...] = jnp.where(kept, 0.0, HIDDEN)


def mask_bias(positions, own, begin):
    return pl.pallas_call(
        bias_kernel,
        out_shape=jax.ShapeDtypeStruct((PACK, ROWS), jnp.float32),
        in_specs=[VMEM] * 3,
        out_specs=VMEM,
        cost_estimate=cost(4 * PACK * ROWS, 4 * PACK * ROWS),
        name="mask_bias",
    )(positions, own, begin)


def attention_kernel(chunk, first, layout, has_start, last, sources, turned_queries, bias, *refs):
    count = sum(layout)
    parts = refs[:count]
    rest = refs[count:]
    if has_start:
        peak_in, total_in, mixed_in = rest[:3]
        rest = rest[3:]
    if last:
        if chunk > 0:
            rest = rest[1:]
        (out,) = rest
    else:
        peak_out, total_out, mixed_out = rest
    scale = math.log2(math.e) / math.sqrt(HEAD_SIZE)
    head = pl.program_id(0)
    local = head // GROUP
    rows = pl.ds(pl.multiple_of(local * HEAD_SIZE, HEAD_SIZE), HEAD_SIZE)
    queries = turned_queries[...]
    scores = []
    values = []
    position = 0
    for i, pieces in enumerate(layout):
        if pieces == 1:
            keys = parts[position][:ROWS, rows]
            below = pl.ds(pl.multiple_of(ROWS + local * HEAD_SIZE, HEAD_SIZE), HEAD_SIZE)
            values.append(parts[position][below, :])
        else:
            keys = parts[position][:, rows]
            values.append(parts[position + 1][rows, :])
        position += pieces
        source = sources[first + i]
        score = jnp.dot(keys, queries, preferred_element_type=jnp.float32)
        scores.append(score + bias[pl.ds(pl.multiple_of(source * ROWS, ROWS), ROWS), :])
    peak = functools.reduce(jnp.maximum, [jnp.max(s, axis=0, keepdims=True) for s in scores])
    if has_start:
        before = peak_in[0]
        peak = jnp.maximum(peak, before)
        shrink = jnp.exp2((before - peak) * scale)
    total = jnp.zeros((1, ROWS), jnp.float32)
    mixed = jnp.zeros((HEAD_SIZE, ROWS), jnp.float32)
    for score, value in zip(scores, values):
        expo = jnp.exp2((score - peak) * scale)
        total = total + jnp.sum(expo, axis=0, keepdims=True)
        mixed = mixed + jnp.dot(
            value, expo.astype(jnp.bfloat16), preferred_element_type=jnp.float32
        )
    if has_start:
        total = total + total_in[0] * shrink
        mixed = mixed + mixed_in[...] * shrink
    if last:
        out[...] = (mixed / total).T.astype(jnp.bfloat16)
    else:
        peak_out[0] = peak
        total_out[0] = total
        mixed_out[...] = mixed


def attention(chunk, first, pieces, sources, turned_queries, bias, start, last, result):
    heads = CHUNK_HEADS * GROUP
    layout = tuple(len(p) for p in pieces)
    parts = [a for p in pieces for a in p]
    whole = lambda a: pl.BlockSpec(a.shape, lambda h: (0, 0))
    row = pl.BlockSpec((1, 1, ROWS), lambda h: (h, 0, 0))
    tall = pl.BlockSpec((HEAD_SIZE, ROWS), lambda h: (h, 0))
    in_specs = [
        SMEM,
        pl.BlockSpec((HEAD_SIZE, ROWS), lambda h: (chunk * heads + h, 0)),
        whole(bias),
    ] + [whole(a) for a in parts]
    operands = [sources, turned_queries, bias] + parts
    if start is not None:
        in_specs += [row, row, tall]
        operands += list(start)
    aliases = {}
    if last:
        if chunk > 0:
            in_specs.append(pl.BlockSpec(memory_space=pl.ANY))
            operands.append(result)
            aliases = {len(operands) - 1: 0}
        out_shape = jax.ShapeDtypeStruct((ROWS, QUERY_HEADS * HEAD_SIZE), jnp.bfloat16)
        out_specs = pl.BlockSpec((ROWS, HEAD_SIZE), lambda h: (0, chunk * heads + h))
    else:
        line = jax.ShapeDtypeStruct((heads, 1, ROWS), jnp.float32)
        out_shape = (line, line, jax.ShapeDtypeStruct((heads * HEAD_SIZE, ROWS), jnp.float32))
        out_specs = (row, row, tall)
    keys = len(layout) * ROWS
    return pl.pallas_call(
        functools.partial(attention_kernel, chunk, first, layout, start is not None, last),
        grid=(heads,),
        out_shape=out_shape,
        in_specs=in_specs,
        out_specs=out_specs,
        input_output_aliases=aliases,
        cost_estimate=cost(
            4 * heads * keys * ROWS * HEAD_SIZE, 8 * heads * HEAD_SIZE * ROWS, heads * keys * ROWS
        ),
        name="attention",
    )(*operands)


def gather_weight(weight):
    near = [weight] + [plane_shift(weight, 0, k) for k in (1, -1, 2)]
    line = jnp.concatenate(near, axis=0)
    left = plane_shift(line, 1, 1)
    right = plane_shift(line, 1, -1)
    half = line.shape[0] // 2
    far = (plane_shift(left[:half], 1, 1), plane_shift(right[half:], 1, -1))
    return line, left, right, far


def gather_keys(pair):
    left = [ring_shift(pair, 1)]
    right = [ring_shift(pair, -1)]
    for _ in range(RING // 2 - 2):
        left.append(ring_shift(left[-1], 1))
        right.append(ring_shift(right[-1], -1))
    far = (ring_shift(left[-1][:ROWS], 1), ring_shift(right[-1][ROWS:], -1))
    return left, right, far


def on_device(hidden_states, queries, norm_gain, key_value_matrix, trace_offsets, token_order):
    device = lax.axis_index("dp")
    place = lax.axis_index("sp")
    core = device % 2
    x = device // (2 * SIDE)
    y = (device // 2) % SIDE

    gathered = [
        gather_weight(key_value_matrix[:, j * CHUNK_COLUMNS : (j + 1) * CHUNK_COLUMNS])
        for j in range(CHUNKS)
    ]

    value_rows = hidden_states[0].astype(jnp.float32)
    scale = lax.rsqrt(jnp.mean(value_rows * value_rows, axis=-1, keepdims=True) + EPSILON)
    normed = (value_rows * scale * norm_gain.astype(jnp.float32)).astype(jnp.bfloat16)
    by_core = normed.reshape(ROWS, CHIPS, 2, ROWS)
    mine = jnp.where(core == 0, by_core[:, :, 0], by_core[:, :, 1]).reshape(ROWS, CHIPS * ROWS)
    other = jnp.where(core == 0, by_core[:, :, 1], by_core[:, :, 0]).reshape(ROWS, CHIPS * ROWS)
    partner = partner_swap(other)

    chips = []
    for second in (0, -1, 1, 2):
        for first in (0, -1, 1, 2):
            along = jnp.where(core == 0, first, second)
            across = jnp.where(core == 0, second, first)
            chips.append(((x + along) % SIDE) * SIDE + (y + across) % SIDE)
    table = jnp.stack(chips).astype(jnp.int32)
    sources = jnp.stack([(place + k) % RING for k in (0, -1, 1, -2, 2, -3, 3, 4)]).astype(jnp.int32)

    starts = trace_offsets[0]
    positions = token_order[0]
    own = lax.dynamic_slice_in_dim(positions, place * ROWS, ROWS, 0)
    inside = starts[None, :] <= own[:, None]
    begin = jnp.max(jnp.where(inside, starts[None, :], 0), axis=1)
    within = own - begin
    half = HEAD_SIZE // 2
    index = jnp.arange(half, dtype=jnp.float32)
    freqs = jnp.exp(index * (-2.0 * math.log(ROPE_BASE) / HEAD_SIZE))
    angles = within.astype(jnp.float32)[:, None] * freqs[None, :]
    cosine = jnp.cos(angles)
    sine = jnp.sin(angles)
    cosine = jnp.concatenate([cosine, cosine], axis=-1)
    sine = jnp.concatenate([-sine, sine], axis=-1)

    turned_queries = rotate_queries(queries[0], cosine, sine)
    bias = mask_bias(positions[:, None], own[None, :], begin[None, :])

    result = None
    for j in range(CHUNKS):
        line, left, right, far = gathered[j]
        start = project(table, mine, partner, (line, left, right), 0)
        here, there = project(table, mine, partner, far, 3 * SIDE, start)
        pair = finish_keys(here, partner_swap(there), cosine, sine)
        lefts, rights, last = gather_keys(pair)
        near = [(pair,), (lefts[0],), (rights[0],), (lefts[1],), (rights[1],)]
        state = attention(j, 0, near, sources, turned_queries, bias, None, False, None)
        distant = [(lefts[2],), (rights[2],), last]
        result = attention(j, 5, distant, sources, turned_queries, bias, state, True, result)
    return result[None]


def solution(mesh):
    return jax.shard_map(
        on_device,
        mesh=mesh,
        in_specs=(
            P("dp", "sp", None),
            P("dp", "sp", None),
            P(),
            P("dp", None),
            P("dp", None),
            P("dp", None),
        ),
        out_specs=P("dp", "sp", None),
        check_vma=False,
    )
```
